128 devices in a mesh: blk: 32 (over x_lo, z, y), vec: 4 (over x_hi, core).
Axes of the slice: x: 4 (x_hi: 2, x_lo: 2; x = x_hi * 2 + x_lo), y: 4, z: 4, core: 2. Of those that a mesh axis runs over, the one named last changes fastest.
Arguments:
- cholesky_factors: bfloat16 [1536, 128, 1024], P(('blk', 'vec')), may hold values from -0.1875 to 0.1875
- walker_green: bfloat16 [32, 128, 1024], P('blk'), may hold values from -8 to 8
Outputs:
- exchange_grad: float32 [32, 128, 1024], P('blk', None, 'vec')
- exchange_energy: float32 [32], P('blk')
The draws below stay inside these ranges and needn't reach their ends.
All inputs are finite; a program needn't handle non-finite values.
Results may differ from the reference program's by a relative error of at most 0.0029.
Values may be sent and summed in bfloat16 or wider, within the bound.
No kernel may reach another device: no remote copies, remote signals or barrier semaphores. Data moves between devices by JAX's collectives and lax.ppermute only.
A program may use at most 64 MiB of HBM per device.

```python
import math
import jax
import jax.numpy as jnp
from jax import lax

NEL = 128
NORB = 1024
VEC_DEV = 12
NCHOL = 1536
WALKERS = 32


def draw_walker_green(key, part):
    base_key, scale_key = jax.random.split(jax.random.fold_in(key, 11))
    entries = jnp.clip(jax.random.normal(base_key, (WALKERS, NEL, NORB), jnp.float32), -4.0, 4.0)
    spread = jnp.exp(jax.random.uniform(scale_key, (WALKERS,), jnp.float32, math.log(0.5), math.log(2.0)))
    return (entries * spread[:, None, None]).astype(jnp.bfloat16)


def shard_levels(key, dims, cuts, least, top_value):
    gain, own = 1.0, jax.random.fold_in(key, 6)
    for position, blocks in cuts:
        heights = jnp.exp(jax.random.uniform(jax.random.fold_in(own, position), (blocks,), jnp.float32, least / len(cuts), top_value / len(cuts)))
        gain = gain * jnp.repeat(heights, dims[position] // blocks).reshape([-1 if axis == position else 1 for axis in range(len(dims))])
    return gain


def normal_values(stream_key, dims, scale, most, cuts=(), dtype=jnp.bfloat16):
    gain = shard_levels(stream_key, dims, cuts, -0.22, 0.18) if cuts else 1.0
    result = jax.random.normal(stream_key, dims, jnp.float32) * scale * gain
    return jnp.minimum(jnp.maximum(result, -most), most).astype(dtype)


def setup_inputs(seed: int = 0) -> dict:
    keys = jax.random.split(jax.random.key(seed), 3)
    cholesky_factors = normal_values(keys[0], (NCHOL, NEL, NORB), NORB ** -0.5, 0.1875, ((0, 128),))
    walker_green = draw_walker_green(jax.random.fold_in(keys[2], 71), 0)
    return {"cholesky_factors": cholesky_factors, "walker_green": walker_green}


def reference(cholesky_factors, walker_green):
    green_f = walker_green.astype(jnp.float32)
    blocks = cholesky_factors.reshape(NCHOL // VEC_DEV, VEC_DEV, NEL, NORB)

    def absorb(running, vector_block):
        vectors_float = vector_block.astype(jnp.float32)
        shared_portion = jnp.einsum('gap,wbp->wgab', vectors_float, green_f)
        rounded_lowprec = lax.optimization_barrier(shared_portion.astype(jnp.bfloat16)).astype(jnp.float32)
        summand_terms = jnp.einsum('vhlr,hrm->vlm', rounded_lowprec, vectors_float)
        return (running + summand_terms, None)
    kernel_sum, unused = lax.scan(absorb, jnp.zeros((WALKERS, NEL, NORB), jnp.float32), blocks)
    energy = -0.5 / (NEL * NCHOL) * lax.optimization_barrier(jnp.sum(kernel_sum * green_f, axis=(1, 2)))
    gradient = kernel_sum / math.sqrt(NCHOL)
    return (gradient, energy)
```

```python
import math

import jax
import jax.numpy as jnp
from jax import lax
from jax.sharding import PartitionSpec as P


AXES = ("blk", "vec")
CHIPS = [(x, y, z, c) for x in range(4) for y in range(4) for z in range(4) for c in range(2)]


def place(x, y, z, c):
    x, y, z = x % 4, y % 4, z % 4
    return ((x % 2) * 16 + z * 4 + y) * 4 + (x // 2) * 2 + c


def route(target, chosen=lambda x, y, z, c: True):
    return [(place(*d), place(*target(*d))) for d in CHIPS if chosen(*d)]


def along_x(step):
    return route(lambda x, y, z, c: (x + step, y, z, c))


def along_f(step):
    return route(lambda x, y, z, c: (x, y, z + step, c) if c else (x, y + step, z, c))


def along_s(step):
    return route(lambda x, y, z, c: (x, y + step, z, c) if c else (x, y, z + step, c))


SWAP = route(lambda x, y, z, c: (x, y, z, 1 - c))
TO_OTHER_PARITY = route(lambda x, y, z, c: (x + 1, y, z, c), lambda x, y, z, c: x % 2 == c)


def send(value, pairs):
    return lax.ppermute(value, AXES, pairs)


def terms(vectors, greens):
    part = jnp.einsum("gap,wbp->wgab", vectors, greens, preferred_element_type=jnp.float32)
    part = part.astype(jnp.bfloat16)
    return jnp.einsum("wglr,grm->wlm", part, vectors, preferred_element_type=jnp.float32)


def shards(cholesky_factors, walker_green):
    f32, bf16 = jnp.float32, jnp.bfloat16
    blk_count = lax.axis_size("blk")
    vec_count = lax.axis_size("vec")
    vector_total = cholesky_factors.shape[0] * blk_count * vec_count
    electrons, orbitals = walker_green.shape[1:]
    quarter = orbitals // 4
    vec = lax.axis_index("vec")
    core = vec % 2
    x_lo = lax.axis_index("blk") // 16
    x_hi = vec // 2

    vectors = jnp.concatenate([cholesky_factors, send(cholesky_factors, SWAP)], axis=0)
    green = jnp.where(core == x_lo, walker_green, send(walker_green, TO_OTHER_PARITY))
    behind, ahead, across = (send(green, along_f(step)) for step in (1, -1, 2))
    row = jnp.concatenate([green, ahead, across, behind], axis=0)
    row_ahead = send(row, along_s(-1))
    row_behind = send(row, along_s(1))
    row_across = send(row, along_s(2))

    total = terms(vectors, row)
    to_ahead = send(terms(vectors, row_ahead).astype(bf16), along_s(1))
    to_behind = send(terms(vectors, row_behind).astype(bf16), along_s(-1))
    to_across = send(terms(vectors, row_across).astype(bf16), along_s(2))
    total = total + to_ahead.astype(f32) + to_behind.astype(f32) + to_across.astype(f32)
    low = total.astype(bf16)
    one = send(low[1], along_f(1))
    three = send(low[3], along_f(-1))
    two = send(low[2], along_f(2))
    mine = total[0] + one.astype(f32) + three.astype(f32) + two.astype(f32)

    energy = jnp.sum(mine * green[0].astype(f32))
    split = mine.reshape(electrons, 2, 2, quarter).transpose(2, 1, 0, 3)
    note = jnp.full((2, 2, 8, quarter), energy, f32)
    split = jnp.concatenate([split, note], axis=2)
    kept = lax.dynamic_index_in_dim(split, core, 0, keepdims=False)
    got = send(lax.dynamic_index_in_dim(split, 1 - core, 0, keepdims=False), SWAP)
    even = jnp.where(core == 0, kept, got)
    odd = jnp.where(core == 0, got, kept)
    same = jnp.where(x_lo == 0, even, odd)
    other = jnp.where(x_lo == 0, odd, even)
    here = lax.dynamic_index_in_dim(same, x_hi, 0, keepdims=False)
    far = lax.dynamic_index_in_dim(same, 1 - x_hi, 0, keepdims=False)
    up_hi = (x_hi + x_lo) % 2
    up = lax.dynamic_index_in_dim(other, up_hi, 0, keepdims=False)
    down = lax.dynamic_index_in_dim(other, 1 - up_hi, 0, keepdims=False)
    whole = here + send(up, along_x(1)) + send(down, along_x(-1)) + send(far, along_x(2))
    gradient = whole[None, :electrons] / math.sqrt(vector_total)
    energy = whole[electrons : electrons + 1, 0] * (-0.5 / (electrons * vector_total))
    return (gradient, energy)


def solution(mesh):
    return jax.shard_map(
        shards,
        mesh=mesh,
        in_specs=(P(("blk", "vec"), None, None), P("blk", None, None)),
        out_specs=(P("blk", None, "vec"), P("blk")),
        check_vma=False,
    )
```

```python
import math

import jax
import jax.numpy as jnp
from jax import lax
from jax.sharding import PartitionSpec as P


AXES = ("blk", "vec")
CHIPS = [(x, y, z, c) for x in range(4) for y in range(4) for z in range(4) for c in range(2)]


def place(x, y, z, c):
    x, y, z = x % 4, y % 4, z % 4
    return ((x % 2) * 16 + z * 4 + y) * 4 + (x // 2) * 2 + c


def route(target, chosen=lambda x, y, z, c: True):
    return [(place(*d), place(*target(*d))) for d in CHIPS if chosen(*d)]


def along_f(step):
    return route(lambda x, y, z, c: (x, y, z + step, c) if c else (x, y + step, z, c))


def along_s(step):
    return route(lambda x, y, z, c: (x, y + step, z, c) if c else (x, y, z + step, c))


SWAP = route(lambda x, y, z, c: (x, y, z, 1 - c))

def first(step, side):
    def target(x, y, z, c):
        core = x % 2
        x = x if c == core else x + side
        return (x, y, z + step, core) if core else (x, y + step, z, core)

    return route(target)


def last(turn):
    def target(x, y, z, c):
        half, other = divmod((x - c + turn) % 4, 2)
        return 2 * half + c, y, z, c ^ other

    return route(target)


def send(value, pairs):
    return lax.ppermute(value, AXES, pairs)


def terms(vectors, greens):
    part = jnp.einsum("gap,wbp->wgab", vectors, greens, preferred_element_type=jnp.float32)
    part = part.astype(jnp.bfloat16)
    return jnp.einsum("wglr,grm->wlm", part, vectors, preferred_element_type=jnp.float32)


def shards(cholesky_factors, walker_green):
    f32, bf16 = jnp.float32, jnp.bfloat16
    blk_count = lax.axis_size("blk")
    vec_count = lax.axis_size("vec")
    vector_total = cholesky_factors.shape[0] * blk_count * vec_count
    electrons, orbitals = walker_green.shape[1:]
    quarter = orbitals // 4
    vec = lax.axis_index("vec")
    core = vec % 2
    x_lo = lax.axis_index("blk") // 16
    x_hi = vec // 2

    partner = send(cholesky_factors, SWAP)
    green = send(walker_green, first(0, 1))
    ahead = send(walker_green, first(-1, -1))
    behind = send(walker_green, first(1, 1))
    across = send(walker_green, first(2, -1))
    row = jnp.concatenate([green, ahead, across, behind], axis=0)
    row, partner = lax.optimization_barrier((row, partner))
    vectors = jnp.concatenate([cholesky_factors, partner], axis=0)
    row_ahead = send(row, along_s(-1))
    row_behind = send(row, along_s(1))
    total = terms(vectors, row)
    row, row_ahead, row_behind, total = lax.optimization_barrier((row, row_ahead, row_behind, total))
    row_across = send(row, along_s(2))

    to_ahead = send(terms(vectors, row_ahead).astype(bf16), along_s(1))
    to_behind = send(terms(vectors, row_behind).astype(bf16), along_s(-1))
    to_across = send(terms(vectors, row_across).astype(bf16), along_s(2))
    total = total + to_ahead.astype(f32) + to_behind.astype(f32) + to_across.astype(f32)
    low = total.astype(bf16)
    one = send(low[1], along_f(1))
    three = send(low[3], along_f(-1))
    two = send(low[2], along_f(2))
    mine = total[0] + one.astype(f32) + three.astype(f32) + two.astype(f32)

    energy = jnp.sum(mine * green[0].astype(f32))
    note = jnp.full((8, orbitals), energy, f32)
    noted = jnp.concatenate([mine, note], axis=0)
    whole = 0.0
    for turn in range(4):
        goal = (2 * x_hi + x_lo - core + turn) % 4
        column = 2 * (goal // 2) + (core + goal) % 2
        piece = lax.dynamic_slice_in_dim(noted, column * quarter, quarter, axis=1)
        whole = whole + send(piece, last(turn))
    gradient = whole[None, :electrons] / math.sqrt(vector_total)
    energy = whole[electrons : electrons + 1, 0] * (-0.5 / (electrons * vector_total))
    return (gradient, energy)


def solution(mesh):
    return jax.shard_map(
        shards,
        mesh=mesh,
        in_specs=(P(("blk", "vec"), None, None), P("blk", None, None)),
        out_specs=(P("blk", None, "vec"), P("blk")),
        check_vma=False,
    )
```

```python
import math

import jax
import jax.numpy as jnp
from jax import lax
from jax.sharding import PartitionSpec as P


AXES = ("blk", "vec")
CHIPS = [(x, y, z, c) for x in range(4) for y in range(4) for z in range(4) for c in range(2)]


def place(x, y, z, c):
    x, y, z = x % 4, y % 4, z % 4
    return ((x % 2) * 16 + z * 4 + y) * 4 + (x // 2) * 2 + c


def route(target, chosen=lambda x, y, z, c: True):
    return [(place(*d), place(*target(*d))) for d in CHIPS if chosen(*d)]


def along_f(step):
    return route(lambda x, y, z, c: (x, y, z + step, c) if c else (x, y + step, z, c))


def along_s(step):
    return route(lambda x, y, z, c: (x, y + step, z, c) if c else (x, y, z + step, c))


SWAP = route(lambda x, y, z, c: (x, y, z, 1 - c))

def first(step, side):
    def target(x, y, z, c):
        core = x % 2
        x = x if c == core else x + side
        return (x, y, z + step, core) if core else (x, y + step, z, core)

    return route(target)


def last(turn):
    def target(x, y, z, c):
        half, other = divmod((x - c + turn) % 4, 2)
        return 2 * half + c, y, z, c ^ other

    return route(target)


def send(value, pairs):
    return lax.ppermute(value, AXES, pairs)


def after(value, *others):
    return lax.optimization_barrier((value, *others))[0]


def intersect(vectors, *greens):
    greens = jnp.concatenate(greens, axis=0) if len(greens) > 1 else greens[0]
    part = jnp.einsum("gap,wbp->wgab", vectors, greens, preferred_element_type=jnp.float32)
    return lax.optimization_barrier(part.astype(jnp.bfloat16))


def terms(part, vectors, kind):
    total = jnp.einsum("wglr,grm->wlm", part, vectors, preferred_element_type=jnp.float32)
    return lax.optimization_barrier(total.astype(kind))


def shards(cholesky_factors, walker_green):
    f32, bf16 = jnp.float32, jnp.bfloat16
    blk_count = lax.axis_size("blk")
    vec_count = lax.axis_size("vec")
    vector_total = cholesky_factors.shape[0] * blk_count * vec_count
    electrons, orbitals = walker_green.shape[1:]
    quarter = orbitals // 4
    vec = lax.axis_index("vec")
    core = vec % 2
    x_lo = lax.axis_index("blk") // 16
    x_hi = vec // 2

    partner = send(cholesky_factors, SWAP)
    green = send(walker_green, first(0, 1))
    ahead = send(walker_green, first(-1, -1))
    behind = send(walker_green, first(1, 1))
    across = send(walker_green, first(2, -1))
    row_a = jnp.concatenate([ahead, across], axis=0)
    row_b = jnp.concatenate([behind, green], axis=0)
    row_a, row_b, partner = lax.optimization_barrier((row_a, row_b, partner))
    vectors = jnp.concatenate([cholesky_factors, partner], axis=0)
    ahead_a = send(row_a, along_s(-1))
    behind_a = send(row_a, along_s(1))
    own = intersect(vectors, row_a, row_b)
    row_b = after(row_b, own)
    ahead_b = send(row_b, along_s(-1))
    behind_b = send(row_b, along_s(1))

    near_a = intersect(vectors, ahead_a, after(behind_a, own))
    out = terms(near_a[:2], vectors, bf16)
    from_ahead_a = send(out, along_s(1))
    near_a = after(near_a, out)
    out = terms(near_a[2:], vectors, bf16)
    from_behind_a = send(out, along_s(-1))
    row, ahead_b, behind_b, out = lax.optimization_barrier(
        (jnp.concatenate([row_a, row_b], axis=0), ahead_b, behind_b, out)
    )
    far = send(row, along_s(2))
    near_b = intersect(vectors, ahead_b, behind_b)
    out = terms(near_b[:2], vectors, bf16)
    from_ahead_b = send(out, along_s(1))
    near_b = after(near_b, out)
    out = terms(near_b[2:], vectors, bf16)
    from_behind_b = send(out, along_s(-1))
    far = intersect(vectors, after(far, out))
    out = terms(far[:2], vectors, bf16)
    from_across_a = send(out, along_s(2))
    far = after(far, out)
    out = terms(far[2:], vectors, bf16)
    from_across_b = send(out, along_s(2))
    own = after(own, out)
    own_a = terms(own[:2], vectors, f32)
    own_b = terms(after(own, own_a)[2:], vectors, f32)

    sum_a = own_a + from_ahead_a.astype(f32) + from_behind_a.astype(f32) + from_across_a.astype(f32)
    low = sum_a.astype(bf16)
    one = send(low[0], along_f(1))
    two = send(low[1], along_f(2))
    sum_b = own_b + from_ahead_b.astype(f32) + from_behind_b.astype(f32) + from_across_b.astype(f32)
    three = send(sum_b[0].astype(bf16), along_f(-1))
    mine = sum_b[1] + one.astype(f32) + two.astype(f32) + three.astype(f32)

    energy = jnp.sum(mine * green[0].astype(f32))
    note = jnp.full((8, orbitals), energy, f32)
    noted = jnp.concatenate([mine, note], axis=0)
    whole = 0.0
    for turn in range(4):
        goal = (2 * x_hi + x_lo - core + turn) % 4
        column = 2 * (goal // 2) + (core + goal) % 2
        piece = lax.dynamic_slice_in_dim(noted, column * quarter, quarter, axis=1)
        whole = whole + send(piece, last(turn))
    gradient = whole[None, :electrons] / math.sqrt(vector_total)
    energy = whole[electrons : electrons + 1, 0] * (-0.5 / (electrons * vector_total))
    return (gradient, energy)


def solution(mesh):
    return jax.shard_map(
        shards,
        mesh=mesh,
        in_specs=(P(("blk", "vec"), None, None), P("blk", None, None)),
        out_specs=(P("blk", None, "vec"), P("blk")),
        check_vma=False,
    )
```

```python
import math

import jax
import jax.numpy as jnp
from jax import lax
from jax.sharding import PartitionSpec as P


AXES = ("blk", "vec")
CHIPS = [(x, y, z, c) for x in range(4) for y in range(4) for z in range(4) for c in range(2)]


def place(x, y, z, c):
    x, y, z = x % 4, y % 4, z % 4
    return ((x % 2) * 16 + z * 4 + y) * 4 + (x // 2) * 2 + c


def route(target, chosen=lambda x, y, z, c: True):
    return [(place(*d), place(*target(*d))) for d in CHIPS if chosen(*d)]


def along_f(step):
    return route(lambda x, y, z, c: (x, y, z + step, c) if c else (x, y + step, z, c))


def along_s(step):
    return route(lambda x, y, z, c: (x, y + step, z, c) if c else (x, y, z + step, c))


SWAP = route(lambda x, y, z, c: (x, y, z, 1 - c))


def first(step, side):
    def target(x, y, z, c):
        core = x % 2
        x = x if c == core else x + side
        return (x, y, z + step, core) if core else (x, y + step, z, core)

    return route(target)


def last(turn):
    def target(x, y, z, c):
        half, other = divmod((x - c + turn) % 4, 2)
        return 2 * half + c, y, z, c ^ other

    return route(target)


def send(value, pairs):
    return lax.ppermute(value, AXES, pairs)


def joined(*parts):
    return jnp.concatenate(parts, axis=0)


def intersect(vectors, greens):
    part = jnp.einsum("gap,wbp->wgab", vectors, greens, preferred_element_type=jnp.float32)
    part = part.astype(jnp.bfloat16)
    return lax.optimization_barrier(part)


def terms(vectors, part, kind=jnp.bfloat16):
    total = jnp.einsum("wglr,grm->wlm", part, vectors, preferred_element_type=jnp.float32)
    total = total.astype(kind)
    return lax.optimization_barrier(total)


def shards(cholesky_factors, walker_green):
    f32, bf16 = jnp.float32, jnp.bfloat16
    blk_count = lax.axis_size("blk")
    vec_count = lax.axis_size("vec")
    vector_total = cholesky_factors.shape[0] * blk_count * vec_count
    electrons, orbitals = walker_green.shape[1:]
    quarter = orbitals // 4
    vec = lax.axis_index("vec")
    core = vec % 2
    x_lo = lax.axis_index("blk") // 16
    x_hi = vec // 2

    partner = send(cholesky_factors, SWAP)
    across = send(walker_green, first(2, -1))
    ahead = send(walker_green, first(-1, -1))
    behind = send(walker_green, first(1, 1))
    green = send(walker_green, first(0, 1))
    row_a, row_b = joined(ahead, across), joined(behind, green)
    row_a, row_b, partner = lax.optimization_barrier((row_a, row_b, partner))
    vectors = joined(cholesky_factors, partner)
    ahead_a = send(row_a, along_s(-1))
    behind_a = send(row_a, along_s(1))
    own = intersect(vectors, joined(row_a, row_b))
    ahead_b = send(row_b, along_s(-1))
    behind_b = send(row_b, along_s(1))
    far = send(joined(row_a, row_b), along_s(2))
    near = terms(vectors, intersect(vectors, joined(ahead_a, behind_a)))
    from_ahead_a = send(near[:2], along_s(1))
    from_behind_a = send(near[2:], along_s(-1))
    near = terms(vectors, intersect(vectors, joined(ahead_b, behind_b)))
    from_ahead_b = send(near[:2], along_s(1))
    from_behind_b = send(near[2:], along_s(-1))
    far = intersect(vectors, far)
    from_far_a = send(terms(vectors, far[:2]), along_s(2))
    from_far_b = send(terms(vectors, far[2:]), along_s(2))
    own_a = terms(vectors, own[:2], f32)
    own_b = terms(vectors, own[2:], f32)

    sum_a = own_a + from_ahead_a.astype(f32) + from_behind_a.astype(f32) + from_far_a.astype(f32)
    low = sum_a.astype(bf16)
    one = send(low[0], along_f(1))
    two = send(low[1], along_f(2))
    sum_b = own_b + from_far_b.astype(f32) + from_ahead_b.astype(f32) + from_behind_b.astype(f32)
    three = send(sum_b[0].astype(bf16), along_f(-1))
    mine = sum_b[1] + one.astype(f32) + two.astype(f32) + three.astype(f32)

    energy = jnp.sum(mine * green[0].astype(f32))
    note = jnp.full((8, orbitals), energy, f32)
    noted = jnp.concatenate([mine, note], axis=0)
    whole = 0.0
    for turn in range(4):
        goal = (2 * x_hi + x_lo - core + turn) % 4
        column = 2 * (goal // 2) + (core + goal) % 2
        piece = lax.dynamic_slice_in_dim(noted, column * quarter, quarter, axis=1)
        whole = whole + send(piece, last(turn))
    gradient = whole[None, :electrons] / math.sqrt(vector_total)
    energy = whole[electrons : electrons + 1, 0] * (-0.5 / (electrons * vector_total))
    return (gradient, energy)


def solution(mesh):
    return jax.shard_map(
        shards,
        mesh=mesh,
        in_specs=(P(("blk", "vec"), None, None), P("blk", None, None)),
        out_specs=(P("blk", None, "vec"), P("blk")),
        check_vma=False,
    )
```

```python
import math

import jax
import jax.numpy as jnp
from jax import lax
from jax.sharding import PartitionSpec as P


AXES = ("blk", "vec")
CHIPS = [(x, y, z, c) for x in range(4) for y in range(4) for z in range(4) for c in range(2)]


def place(x, y, z, c):
    x, y, z = x % 4, y % 4, z % 4
    return ((x % 2) * 16 + z * 4 + y) * 4 + (x // 2) * 2 + c


def route(target, chosen=lambda x, y, z, c: True):
    return [(place(*d), place(*target(*d))) for d in CHIPS if chosen(*d)]


def along_f(step):
    return route(lambda x, y, z, c: (x, y, z + step, c) if c else (x, y + step, z, c))


def along_s(step):
    return route(lambda x, y, z, c: (x, y + step, z, c) if c else (x, y, z + step, c))


SWAP = route(lambda x, y, z, c: (x, y, z, 1 - c))


def first(step, side):
    def target(x, y, z, c):
        core = x % 2
        x = x if c == core else x + side
        return (x, y, z + step, core) if core else (x, y + step, z, core)

    return route(target)


def last(turn):
    def target(x, y, z, c):
        half, other = divmod((x - c + turn) % 4, 2)
        return 2 * half + c, y, z, c ^ other

    return route(target)


def send(value, pairs):
    return lax.ppermute(value, AXES, pairs)


def joined(*parts):
    return jnp.concatenate(parts, axis=0)


def intersect(vectors, greens):
    part = jnp.einsum("gap,wbp->wgab", vectors, greens, preferred_element_type=jnp.float32)
    part = part.astype(jnp.bfloat16)
    return lax.optimization_barrier(part)


def terms(vectors, part, kind=jnp.bfloat16):
    total = jnp.einsum("wglr,grm->wlm", part, vectors, preferred_element_type=jnp.float32)
    total = total.astype(kind)
    return lax.optimization_barrier(total)


def shards(cholesky_factors, walker_green):
    f32, bf16 = jnp.float32, jnp.bfloat16
    blk_count = lax.axis_size("blk")
    vec_count = lax.axis_size("vec")
    vector_total = cholesky_factors.shape[0] * blk_count * vec_count
    electrons, orbitals = walker_green.shape[1:]
    quarter = orbitals // 4
    vec = lax.axis_index("vec")
    core = vec % 2
    x_lo = lax.axis_index("blk") // 16
    x_hi = vec // 2

    partner = send(cholesky_factors, SWAP)
    across = send(walker_green, first(2, -1))
    ahead = send(walker_green, first(-1, -1))
    behind = send(walker_green, first(1, 1))
    green = send(walker_green, first(0, 1))
    row_a, row_b = joined(ahead, across), joined(behind, green)
    row_a, row_b, partner = lax.optimization_barrier((row_a, row_b, partner))
    vectors = joined(cholesky_factors, partner)
    ahead_a = send(row_a, along_s(-1))
    behind_b = send(row_b, along_s(1))
    own = intersect(vectors, joined(row_a, row_b))
    far_a = send(ahead_a, along_s(-1))
    far_b = send(behind_b, along_s(1))
    y_terms = terms(vectors, intersect(vectors, joined(ahead_a, behind_b)), f32)
    ahead_b = send(row_b, along_s(-1))
    behind_a = send(row_a, along_s(1))
    far_terms = terms(vectors, intersect(vectors, joined(far_a, far_b)))
    via_a = send(far_terms[:2], along_s(1))
    via_b = send(far_terms[2:], along_s(-1))
    x_terms = terms(vectors, intersect(vectors, joined(ahead_b, behind_a)))
    from_ahead_b = send(x_terms[:2], along_s(1))
    from_behind_a = send(x_terms[2:], along_s(-1))
    from_ahead_a = send((y_terms[:2] + via_a.astype(f32)).astype(bf16), along_s(1))
    from_behind_b = send((y_terms[2:] + via_b.astype(f32)).astype(bf16), along_s(-1))
    own = terms(vectors, own, f32)

    sum_a = own[:2] + from_ahead_a.astype(f32) + from_behind_a.astype(f32)
    sum_b = own[2:] + from_ahead_b.astype(f32) + from_behind_b.astype(f32)
    one = send(sum_a[0].astype(bf16), along_f(1))
    three = send(sum_b[0].astype(bf16), along_f(-1))
    two = send(sum_a[1].astype(bf16), along_f(2))
    mine = sum_b[1] + one.astype(f32) + two.astype(f32) + three.astype(f32)

    energy = jnp.sum(mine * green[0].astype(f32))
    note = jnp.full((8, orbitals), energy, f32)
    noted = jnp.concatenate([mine, note], axis=0)
    whole = 0.0
    for turn in range(4):
        goal = (2 * x_hi + x_lo - core + turn) % 4
        column = 2 * (goal // 2) + (core + goal) % 2
        piece = lax.dynamic_slice_in_dim(noted, column * quarter, quarter, axis=1)
        whole = whole + send(piece, last(turn))
    gradient = whole[None, :electrons] / math.sqrt(vector_total)
    energy = whole[electrons : electrons + 1, 0] * (-0.5 / (electrons * vector_total))
    return (gradient, energy)


def solution(mesh):
    return jax.shard_map(
        shards,
        mesh=mesh,
        in_specs=(P(("blk", "vec"), None, None), P("blk", None, None)),
        out_specs=(P("blk", None, "vec"), P("blk")),
        check_vma=False,
    )
```

```python
import math

import jax
import jax.numpy as jnp
from jax import lax
from jax.sharding import PartitionSpec as P


AXES = ("blk", "vec")
CHIPS = [(x, y, z, c) for x in range(4) for y in range(4) for z in range(4) for c in range(2)]


def place(x, y, z, c):
    x, y, z = x % 4, y % 4, z % 4
    return ((x % 2) * 16 + z * 4 + y) * 4 + (x // 2) * 2 + c


def route(target, chosen=lambda x, y, z, c: True):
    return [(place(*d), place(*target(*d))) for d in CHIPS if chosen(*d)]


def along_y(step, x, y, z, c):
    return x, y + step, z, c


def along_z(step, x, y, z, c):
    return x, y, z + step, c


def along_f(step):
    return route(lambda x, y, z, c: (along_y if x % 2 == c else along_z)(step, x, y, z, c))


def along_s(step):
    return route(lambda x, y, z, c: (along_z if x % 2 == c else along_y)(step, x, y, z, c))


SWAP = route(lambda x, y, z, c: (x, y, z, 1 - c))


def first(step, side):
    def target(x, y, z, c):
        if x % 2 == c:
            return along_y(step, x, y, z, c)
        return along_z(step, x + side, y, z, x % 2)

    return route(target)


def last(turn):
    def target(x, y, z, c):
        half, other = divmod((x - c + turn) % 4, 2)
        return 2 * half + c, y, z, c ^ other

    return route(target)


def send(value, pairs):
    return lax.ppermute(value, AXES, pairs)


def joined(*parts):
    return jnp.concatenate(parts, axis=0)


def intersect(vectors, greens):
    part = jnp.einsum("gap,wbp->wgab", vectors, greens, preferred_element_type=jnp.float32)
    part = part.astype(jnp.bfloat16)
    return lax.optimization_barrier(part)


def terms(vectors, part, kind=jnp.bfloat16):
    total = jnp.einsum("wglr,grm->wlm", part, vectors, preferred_element_type=jnp.float32)
    total = total.astype(kind)
    return lax.optimization_barrier(total)


def shards(cholesky_factors, walker_green):
    f32, bf16 = jnp.float32, jnp.bfloat16
    blk_count = lax.axis_size("blk")
    vec_count = lax.axis_size("vec")
    vector_total = cholesky_factors.shape[0] * blk_count * vec_count
    electrons, orbitals = walker_green.shape[1:]
    quarter = orbitals // 4
    vec = lax.axis_index("vec")
    core = vec % 2
    x_lo = lax.axis_index("blk") // 16
    x_hi = vec // 2

    partner = send(cholesky_factors, SWAP)
    across = send(walker_green, first(2, -1))
    ahead = send(walker_green, first(-1, -1))
    behind = send(walker_green, first(1, 1))
    green = send(walker_green, first(0, 1))
    row_a, row_b = joined(ahead, across), joined(behind, green)
    row_a, row_b, partner = lax.optimization_barrier((row_a, row_b, partner))
    vectors = joined(cholesky_factors, partner)
    ahead_a = send(row_a, along_s(-1))
    behind_b = send(row_b, along_s(1))
    own = intersect(vectors, joined(row_a, row_b))
    far_a = send(ahead_a, along_s(-1))
    far_b = send(behind_b, along_s(1))
    y_terms = terms(vectors, intersect(vectors, joined(ahead_a, behind_b)), f32)
    ahead_b = send(row_b, along_s(-1))
    behind_a = send(row_a, along_s(1))
    far_terms = terms(vectors, intersect(vectors, joined(far_a, far_b)))
    via_a = send(far_terms[:2], along_s(1))
    via_b = send(far_terms[2:], along_s(-1))
    x_terms = terms(vectors, intersect(vectors, joined(ahead_b, behind_a)))
    from_ahead_b = send(x_terms[:2], along_s(1))
    from_behind_a = send(x_terms[2:], along_s(-1))
    from_ahead_a = send((y_terms[:2] + via_a.astype(f32)).astype(bf16), along_s(1))
    from_behind_b = send((y_terms[2:] + via_b.astype(f32)).astype(bf16), along_s(-1))
    own = terms(vectors, own, f32)

    sum_a = own[:2] + from_ahead_a.astype(f32) + from_behind_a.astype(f32)
    sum_b = own[2:] + from_ahead_b.astype(f32) + from_behind_b.astype(f32)
    one = send(sum_a[0].astype(bf16), along_f(1))
    three = send(sum_b[0].astype(bf16), along_f(-1))
    two = send(sum_a[1].astype(bf16), along_f(2))
    mine = sum_b[1] + one.astype(f32) + two.astype(f32) + three.astype(f32)

    energy = jnp.sum(mine * green[0].astype(f32))
    note = jnp.full((8, orbitals), energy, f32)
    noted = jnp.concatenate([mine, note], axis=0)
    pieces = []
    for turn in range(4):
        goal = (2 * x_hi + x_lo - core + turn) % 4
        column = 2 * (goal // 2) + (core + goal) % 2
        piece = lax.dynamic_slice_in_dim(noted, column * quarter, quarter, axis=1)
        pieces.append(send(piece, last(turn)))
    gradient = sum(piece[None, :electrons] for piece in pieces) / math.sqrt(vector_total)
    energy = sum(piece[electrons, :1] for piece in pieces) * (-0.5 / (electrons * vector_total))
    return (gradient, energy)


def solution(mesh):
    return jax.shard_map(
        shards,
        mesh=mesh,
        in_specs=(P(("blk", "vec"), None, None), P("blk", None, None)),
        out_specs=(P("blk", None, "vec"), P("blk")),
        check_vma=False,
    )
```

```python
import math

import jax
import jax.numpy as jnp
from jax import lax
from jax.sharding import PartitionSpec as P


AXES = ("blk", "vec")
CHIPS = [(x, y, z, c) for x in range(4) for y in range(4) for z in range(4) for c in range(2)]


def place(x, y, z, c):
    x, y, z = x % 4, y % 4, z % 4
    return ((x % 2) * 16 + z * 4 + y) * 4 + (x // 2) * 2 + c


def route(target, chosen=lambda x, y, z, c: True):
    return [(place(*d), place(*target(*d))) for d in CHIPS if chosen(*d)]


def along_f(step):
    return route(lambda x, y, z, c: (x, y, z + step, c) if c else (x, y + step, z, c))


def along_s(step):
    return route(lambda x, y, z, c: (x, y + step, z, c) if c else (x, y, z + step, c))


SWAP = route(lambda x, y, z, c: (x, y, z, 1 - c))


def first(step, side):
    return route(lambda x, y, z, c: (x + side, y, z + step, c) if c else (x, y + step, z, c))


def goal(turn, x, c):
    return (x - (x + c) % 2 + turn) % 4


def last(turn):
    def target(x, y, z, c):
        half, core = goal(turn, x, c) // 2, goal(turn, x, c) % 2
        return 2 * half + (x + c) % 2, y, z, core

    return route(target)


def send(value, pairs):
    return lax.ppermute(value, AXES, pairs)


def joined(*parts):
    return jnp.concatenate(parts, axis=0)


def intersect(vectors, greens):
    part = jnp.einsum("gap,wbp->wgab", vectors, greens, preferred_element_type=jnp.float32)
    part = part.astype(jnp.bfloat16)
    return lax.optimization_barrier(part)


def terms(vectors, part, kind=jnp.bfloat16):
    total = jnp.einsum("wglr,grm->wlm", part, vectors, preferred_element_type=jnp.float32)
    total = total.astype(kind)
    return lax.optimization_barrier(total)


def shards(cholesky_factors, walker_green):
    f32, bf16 = jnp.float32, jnp.bfloat16
    blk_count = lax.axis_size("blk")
    vec_count = lax.axis_size("vec")
    vector_total = cholesky_factors.shape[0] * blk_count * vec_count
    electrons, orbitals = walker_green.shape[1:]
    quarter = orbitals // 4
    vec = lax.axis_index("vec")
    core = vec % 2
    x_lo = lax.axis_index("blk") // 16
    x_hi = vec // 2

    partner = send(cholesky_factors, SWAP)
    across = send(walker_green, first(2, -1))
    ahead = send(walker_green, first(-1, -1))
    behind = send(walker_green, first(1, 1))
    green = send(walker_green, first(0, 1))
    row_a, row_b = joined(ahead, across), joined(behind, green)
    row_a, row_b, partner = lax.optimization_barrier((row_a, row_b, partner))
    vectors = joined(cholesky_factors, partner)
    ahead_a = send(row_a, along_s(-1))
    behind_b = send(row_b, along_s(1))
    own = intersect(vectors, joined(row_a, row_b))
    far_a = send(ahead_a, along_s(-1))
    far_b = send(behind_b, along_s(1))
    y_terms = terms(vectors, intersect(vectors, joined(ahead_a, behind_b)), f32)
    ahead_b = send(row_b, along_s(-1))
    behind_a = send(row_a, along_s(1))
    far_terms = terms(vectors, intersect(vectors, joined(far_a, far_b)))
    via_a = send(far_terms[:2], along_s(1))
    via_b = send(far_terms[2:], along_s(-1))
    x_terms = terms(vectors, intersect(vectors, joined(ahead_b, behind_a)))
    from_ahead_b = send(x_terms[:2], along_s(1))
    from_behind_a = send(x_terms[2:], along_s(-1))
    from_ahead_a = send((y_terms[:2] + via_a.astype(f32)).astype(bf16), along_s(1))
    from_behind_b = send((y_terms[2:] + via_b.astype(f32)).astype(bf16), along_s(-1))
    own = terms(vectors, own, f32)

    sum_a = own[:2] + from_ahead_a.astype(f32) + from_behind_a.astype(f32)
    sum_b = own[2:] + from_ahead_b.astype(f32) + from_behind_b.astype(f32)
    one = send(sum_a[0].astype(bf16), along_f(1))
    three = send(sum_b[0].astype(bf16), along_f(-1))
    two = send(sum_a[1].astype(bf16), along_f(2))
    mine = sum_b[1] + one.astype(f32) + two.astype(f32) + three.astype(f32)

    energy = jnp.sum(mine * green[0].astype(f32))
    note = jnp.full((8, orbitals), energy, f32)
    noted = jnp.concatenate([mine, note], axis=0)
    whole = 0.0
    for turn in range(4):
        column = goal(turn, 2 * x_hi + x_lo, core) * quarter
        piece = lax.dynamic_slice_in_dim(noted, column, quarter, axis=1)
        whole = whole + send(piece, last(turn))
    gradient = whole[None, :electrons] / math.sqrt(vector_total)
    energy = whole[electrons, :1] * (-0.5 / (electrons * vector_total))
    return (gradient, energy)


def solution(mesh):
    return jax.shard_map(
        shards,
        mesh=mesh,
        in_specs=(P(("blk", "vec"), None, None), P("blk", None, None)),
        out_specs=(P("blk", None, "vec"), P("blk")),
        check_vma=False,
    )
```

```python
import math

import jax
import jax.numpy as jnp
from jax import lax
from jax.sharding import PartitionSpec as P


AXES = ("blk", "vec")
CHIPS = [(x, y, z, c) for x in range(4) for y in range(4) for z in range(4) for c in range(2)]


def place(x, y, z, c):
    x, y, z = x % 4, y % 4, z % 4
    return ((x % 2) * 16 + z * 4 + y) * 4 + (x // 2) * 2 + c


def route(target, chosen=lambda x, y, z, c: True):
    return [(place(*d), place(*target(*d))) for d in CHIPS if chosen(*d)]


def along_f(step):
    return route(lambda x, y, z, c: (x, y, z + step, c) if c else (x, y + step, z, c))


def along_s(step):
    return route(lambda x, y, z, c: (x, y + step, z, c) if c else (x, y, z + step, c))


SWAP = route(lambda x, y, z, c: (x, y, z, 1 - c))


def first(step, side):
    return route(lambda x, y, z, c: (x + side, y, z + step, c) if c else (x, y + step, z, c))


def goal(turn, x, c):
    return (x - (x + c) % 2 + turn) % 4


def last(turn):
    def target(x, y, z, c):
        half, core = goal(turn, x, c) // 2, goal(turn, x, c) % 2
        return 2 * half + (x + c) % 2, y, z, core

    return route(target)


def send(value, pairs):
    return lax.ppermute(value, AXES, pairs)


def joined(*parts):
    return jnp.concatenate(parts, axis=0)


def intersect(vectors, greens):
    part = jnp.einsum("gap,wbp->wgab", vectors, greens, preferred_element_type=jnp.float32)
    part = part.astype(jnp.bfloat16)
    return lax.optimization_barrier(part)


def terms(vectors, part, kind=jnp.bfloat16):
    total = jnp.einsum("wglr,grm->wlm", part, vectors, preferred_element_type=jnp.float32)
    total = total.astype(kind)
    return lax.optimization_barrier(total)


def shards(cholesky_factors, walker_green):
    f32, bf16 = jnp.float32, jnp.bfloat16
    blk_count = lax.axis_size("blk")
    vec_count = lax.axis_size("vec")
    vector_total = cholesky_factors.shape[0] * blk_count * vec_count
    electrons, orbitals = walker_green.shape[1:]
    quarter = orbitals // 4
    vec = lax.axis_index("vec")
    core = vec % 2
    x_lo = lax.axis_index("blk") // 16
    x_hi = vec // 2

    partner = send(cholesky_factors, SWAP)
    across = send(walker_green, first(2, -1))
    ahead = send(walker_green, first(-1, -1))
    behind = send(walker_green, first(1, 1))
    green = send(walker_green, first(0, 1))
    row_a, row_b = joined(ahead, across), joined(behind, green)
    vectors = lax.optimization_barrier(joined(cholesky_factors, partner))
    ahead_a = send(row_a, along_s(-1))
    behind_b = send(row_b, along_s(1))
    own = intersect(vectors, joined(across, behind, ahead, green))
    far_a = send(ahead_a, along_s(-1))
    far_b = send(behind_b, along_s(1))
    y_terms = terms(vectors, intersect(vectors, joined(ahead_a, behind_b)), f32)
    ahead_b = send(row_b, along_s(-1))
    behind_a = send(row_a, along_s(1))
    far_terms = terms(vectors, intersect(vectors, joined(far_a, far_b)))
    via_a = send(far_terms[:2], along_s(1))
    via_b = send(far_terms[2:], along_s(-1))
    x_terms = terms(vectors, intersect(vectors, joined(ahead_b, behind_a)))
    from_ahead_b = send(x_terms[:2], along_s(1))
    from_behind_a = send(x_terms[2:], along_s(-1))
    y_ahead = (y_terms[:2] + via_a.astype(f32)).astype(bf16)
    y_behind = (y_terms[2:] + via_b.astype(f32)).astype(bf16)
    y_two = send(y_ahead[1], along_s(1))
    y_three = send(y_behind[0], along_s(-1))
    y_one = send(y_ahead[0], along_s(1))
    y_zero = send(y_behind[1], along_s(-1))

    total = terms(vectors, own[:2], f32)
    two = (total[0] + y_two.astype(f32) + from_behind_a[1].astype(f32)).astype(bf16)
    three = (total[1] + y_three.astype(f32) + from_ahead_b[0].astype(f32)).astype(bf16)
    own, _, _ = lax.optimization_barrier((own, two, three))
    two = send(two, along_f(2))
    three = send(three, along_f(-1))
    total = terms(vectors, own[2:], f32)
    one = (total[0] + y_one.astype(f32) + from_behind_a[0].astype(f32)).astype(bf16)
    one = send(one, along_f(1))
    mine = total[1] + y_zero.astype(f32) + from_ahead_b[1].astype(f32)
    mine = mine + one.astype(f32) + two.astype(f32) + three.astype(f32)

    energy = jnp.sum(mine * green[0].astype(f32))
    note = jnp.full((8, orbitals), energy, f32)
    noted = jnp.concatenate([mine, note], axis=0)
    whole = 0.0
    for turn in range(4):
        column = goal(turn, 2 * x_hi + x_lo, core) * quarter
        piece = lax.dynamic_slice_in_dim(noted, column, quarter, axis=1)
        whole = whole + send(piece, last(turn))
    gradient = whole[None, :electrons] / math.sqrt(vector_total)
    energy = whole[electrons, :1] * (-0.5 / (electrons * vector_total))
    return (gradient, energy)


def solution(mesh):
    return jax.shard_map(
        shards,
        mesh=mesh,
        in_specs=(P(("blk", "vec"), None, None), P("blk", None, None)),
        out_specs=(P("blk", None, "vec"), P("blk")),
        check_vma=False,
    )
```

```python
import functools
import math

import jax
import jax.numpy as jnp
from jax import lax
from jax.experimental import pallas as pl
from jax.experimental.pallas import tpu as pltpu
from jax.sharding import PartitionSpec as P


AXES = ("blk", "vec")
CHIPS = [(x, y, z, c) for x in range(4) for y in range(4) for z in range(4) for c in range(2)]


def place(x, y, z, c):
    x, y, z = x % 4, y % 4, z % 4
    return ((x % 2) * 16 + z * 4 + y) * 4 + (x // 2) * 2 + c


def route(target, chosen=lambda x, y, z, c: True):
    return [(place(*d), place(*target(*d))) for d in CHIPS if chosen(*d)]


def along_f(step):
    return route(lambda x, y, z, c: (x, y, z + step, c) if c else (x, y + step, z, c))


def along_s(step):
    return route(lambda x, y, z, c: (x, y + step, z, c) if c else (x, y, z + step, c))


SWAP = route(lambda x, y, z, c: (x, y, z, 1 - c))


def first(step, side):
    return route(lambda x, y, z, c: (x + side, y, z + step, c) if c else (x, y + step, z, c))


def goal(turn, x, c):
    return (x - (x + c) % 2 + turn) % 4


def last(turn):
    def target(x, y, z, c):
        half, core = goal(turn, x, c) // 2, goal(turn, x, c) % 2
        return 2 * half + (x + c) % 2, y, z, core

    return route(target)


def send(value, pairs):
    return lax.ppermute(value, AXES, pairs)


def joined(*parts):
    return jnp.concatenate(parts, axis=0)


def intersect(vectors, greens):
    part = jnp.einsum("gap,wbp->wgab", vectors, greens, preferred_element_type=jnp.float32)
    part = part.astype(jnp.bfloat16)
    return lax.optimization_barrier(part)


def terms(vectors, part, kind=jnp.bfloat16):
    total = jnp.einsum("wglr,grm->wlm", part, vectors, preferred_element_type=jnp.float32)
    total = total.astype(kind)
    return lax.optimization_barrier(total)


KINDS = (jnp.float32, jnp.float32, jnp.bfloat16, jnp.bfloat16)
NOTE = (8, 8, 16, 16)


def close_kernel(base, zero, one, two, three, green, *rest):
    pieces, total = rest[:4], rest[4]
    electrons, orbitals = zero.shape
    quarter = orbitals // 4
    products = jnp.zeros((electrons, quarter), jnp.float32)
    for column in range(4):
        block = slice(column * quarter, (column + 1) * quarter)
        value = zero[:, block] + one[:, block].astype(jnp.float32)
        value = value + two[:, block].astype(jnp.float32) + three[:, block].astype(jnp.float32)
        total[:, block] = value
        products = products + value * green[:, block].astype(jnp.float32)
    energy = jnp.full((16, quarter), jnp.sum(products), jnp.float32)
    high = energy.astype(jnp.bfloat16).astype(jnp.float32)
    middle = (energy - high).astype(jnp.bfloat16).astype(jnp.float32)
    low = energy - high - middle
    line = lax.broadcasted_iota(jnp.int32, energy.shape, 0)
    parts = jnp.where(line == 0, high, jnp.where(line == 1, middle, jnp.where(line == 2, low, 0.0)))
    for turn, piece in enumerate(pieces):
        start = pl.multiple_of(((base[0] + turn) & 3) * quarter, quarter)
        piece[:electrons, :] = total[:, pl.ds(start, quarter)].astype(piece.dtype)
        if piece.dtype == jnp.float32:
            piece[electrons:, :] = energy[:8]
        else:
            piece[electrons:, :] = parts.astype(piece.dtype)


def close(base, zero, one, two, three, green):
    electrons, orbitals = zero.shape
    vmem = pl.BlockSpec(memory_space=pltpu.VMEM)
    return pl.pallas_call(
        close_kernel,
        out_shape=[
            jax.ShapeDtypeStruct((electrons + lines, orbitals // 4), kind)
            for lines, kind in zip(NOTE, KINDS)
        ],
        in_specs=[pl.BlockSpec(memory_space=pltpu.SMEM)] + [vmem] * 5,
        out_specs=[vmem] * 4,
        scratch_shapes=[pltpu.VMEM((electrons, orbitals), jnp.float32)],
        compiler_params=pltpu.CompilerParams(vmem_limit_bytes=8 << 20),
        name="close",
    )(base, zero, one, two, three, green)


def finish_kernel(root, factor, p0, p1, p2, p3, gradient, energy):
    electrons = gradient.shape[1]
    total, note = 0.0, 0.0
    for piece in (p0, p1, p2, p3):
        total = total + piece[:electrons, :].astype(jnp.float32)
        if piece.dtype == jnp.float32:
            note = note + piece[electrons : electrons + 1, :]
        else:
            note = note + jnp.sum(piece[electrons:, :].astype(jnp.float32), axis=0, keepdims=True)
    gradient[0] = total / root
    energy[0] = jnp.max(note) * factor


def finish(pieces, root, factor):
    electrons = pieces[0].shape[0] - NOTE[0]
    vmem = pl.BlockSpec(memory_space=pltpu.VMEM)
    return pl.pallas_call(
        functools.partial(finish_kernel, root, factor),
        out_shape=[
            jax.ShapeDtypeStruct((1, electrons, pieces[0].shape[1]), jnp.float32),
            jax.ShapeDtypeStruct((1,), jnp.float32),
        ],
        in_specs=[vmem] * 4,
        out_specs=[vmem, pl.BlockSpec(memory_space=pltpu.SMEM)],
        compiler_params=pltpu.CompilerParams(vmem_limit_bytes=8 << 20),
        name="finish",
    )(*pieces)


def shards(cholesky_factors, walker_green):
    f32, bf16 = jnp.float32, jnp.bfloat16
    blk_count = lax.axis_size("blk")
    vec_count = lax.axis_size("vec")
    vector_total = cholesky_factors.shape[0] * blk_count * vec_count
    electrons, _ = walker_green.shape[1:]
    vec = lax.axis_index("vec")
    core = vec % 2
    x_lo = lax.axis_index("blk") // 16
    x_hi = vec // 2

    partner = send(cholesky_factors, SWAP)
    across = send(walker_green, first(2, -1))
    ahead = send(walker_green, first(-1, -1))
    behind = send(walker_green, first(1, 1))
    green = send(walker_green, first(0, 1))
    row_a, row_b = joined(ahead, across), joined(behind, green)
    vectors = lax.optimization_barrier(joined(cholesky_factors, partner))
    ahead_a = send(row_a, along_s(-1))
    behind_b = send(row_b, along_s(1))
    own = intersect(vectors, joined(across, behind, ahead, green))
    far_a = send(ahead_a, along_s(-1))
    far_b = send(behind_b, along_s(1))
    y_terms = terms(vectors, intersect(vectors, joined(ahead_a, behind_b)), f32)
    ahead_b = send(row_b, along_s(-1))
    behind_a = send(row_a, along_s(1))
    far_terms = terms(vectors, intersect(vectors, joined(far_a, far_b)))
    via_a = send(far_terms[:2], along_s(1))
    via_b = send(far_terms[2:], along_s(-1))
    x_terms = terms(vectors, intersect(vectors, joined(ahead_b, behind_a)))
    from_ahead_b = send(x_terms[:2], along_s(1))
    from_behind_a = send(x_terms[2:], along_s(-1))
    y_ahead = (y_terms[:2] + via_a.astype(f32)).astype(bf16)
    y_behind = (y_terms[2:] + via_b.astype(f32)).astype(bf16)
    y_two = send(y_ahead[1], along_s(1))
    y_three = send(y_behind[0], along_s(-1))
    y_one = send(y_ahead[0], along_s(1))
    y_zero = send(y_behind[1], along_s(-1))

    total = terms(vectors, own[:2], f32)
    two = (total[0] + y_two.astype(f32) + from_behind_a[1].astype(f32)).astype(bf16)
    three = (total[1] + y_three.astype(f32) + from_ahead_b[0].astype(f32)).astype(bf16)
    own, _, _ = lax.optimization_barrier((own, two, three))
    two = send(two, along_f(2))
    three = send(three, along_f(-1))
    total = terms(vectors, own[2:], f32)
    one = (total[0] + y_one.astype(f32) + from_behind_a[0].astype(f32)).astype(bf16)
    one = send(one, along_f(1))
    zero = total[1] + y_zero.astype(f32) + from_ahead_b[1].astype(f32)
    base = (2 * x_hi + x_lo + 4 - (x_lo ^ core)) & 3
    pieces = close(base.reshape(1), zero, one, two, three, green[0])
    pieces = [send(pieces[turn], last(turn)) for turn in range(4)]
    gradient, energy = finish(pieces, math.sqrt(vector_total), -0.5 / (electrons * vector_total))
    return (gradient, energy)


def solution(mesh):
    return jax.shard_map(
        shards,
        mesh=mesh,
        in_specs=(P(("blk", "vec"), None, None), P("blk", None, None)),
        out_specs=(P("blk", None, "vec"), P("blk")),
        check_vma=False,
    )
```

```python
import functools
import math

import jax
import jax.numpy as jnp
from jax import lax
from jax.experimental import pallas as pl
from jax.experimental.pallas import tpu as pltpu
from jax.sharding import PartitionSpec as P


AXES = ("blk", "vec")
CHIPS = [(x, y, z, c) for x in range(4) for y in range(4) for z in range(4) for c in range(2)]


def place(x, y, z, c):
    x, y, z = x % 4, y % 4, z % 4
    return ((x % 2) * 16 + z * 4 + y) * 4 + (x // 2) * 2 + c


def route(target, chosen=lambda x, y, z, c: True):
    return [(place(*d), place(*target(*d))) for d in CHIPS if chosen(*d)]


def along_f(step):
    return route(lambda x, y, z, c: (x, y, z + step, c) if c else (x, y + step, z, c))


def along_s(step):
    return route(lambda x, y, z, c: (x, y + step, z, c) if c else (x, y, z + step, c))


SWAP = route(lambda x, y, z, c: (x, y, z, 1 - c))


def first(step, side):
    return route(lambda x, y, z, c: (x + side, y, z + step, c) if c else (x, y + step, z, c))


def goal(turn, x, c):
    return (x - (x + c) % 2 + turn) % 4


def last(turn):
    def target(x, y, z, c):
        half, core = goal(turn, x, c) // 2, goal(turn, x, c) % 2
        return 2 * half + (x + c) % 2, y, z, core

    return route(target)


def send(value, pairs):
    return lax.ppermute(value, AXES, pairs)


def joined(*parts):
    return jnp.concatenate(parts, axis=0)


def intersect(vectors, greens):
    part = jnp.einsum("gap,wbp->wgab", vectors, greens, preferred_element_type=jnp.float32)
    part = part.astype(jnp.bfloat16)
    return lax.optimization_barrier(part)


def terms(vectors, part, kind=jnp.bfloat16):
    total = jnp.einsum("wglr,grm->wlm", part, vectors, preferred_element_type=jnp.float32)
    total = total.astype(kind)
    return lax.optimization_barrier(total)


KINDS = (jnp.float32, jnp.float32, jnp.bfloat16, jnp.bfloat16)
NOTE = (8, 8, 16, 16)


def pair_kernel(first_ref, second_ref, out_ref):
    out_ref[:1] = first_ref[...]
    out_ref[1:] = second_ref[...]


def pair(one, two):
    vmem = pl.BlockSpec(memory_space=pltpu.VMEM)
    return pl.pallas_call(
        pair_kernel,
        out_shape=jax.ShapeDtypeStruct((2, *one.shape[1:]), one.dtype),
        in_specs=[vmem] * 2,
        out_specs=vmem,
        compiler_params=pltpu.CompilerParams(vmem_limit_bytes=8 << 20),
        name="pair",
    )(one, two)


def close_kernel(base, zero, one, two, three, green, *rest):
    pieces, total = rest[:4], rest[4]
    electrons, orbitals = zero.shape
    quarter = orbitals // 4
    products = jnp.zeros((electrons, quarter), jnp.float32)
    for column in range(4):
        block = slice(column * quarter, (column + 1) * quarter)
        value = zero[:, block] + one[:, block].astype(jnp.float32)
        value = value + two[:, block].astype(jnp.float32) + three[:, block].astype(jnp.float32)
        total[:, block] = value
        products = products + value * green[:, block].astype(jnp.float32)
    energy = jnp.full((16, quarter), jnp.sum(products), jnp.float32)
    high = energy.astype(jnp.bfloat16).astype(jnp.float32)
    middle = (energy - high).astype(jnp.bfloat16).astype(jnp.float32)
    low = energy - high - middle
    line = lax.broadcasted_iota(jnp.int32, energy.shape, 0)
    parts = jnp.where(line == 0, high, jnp.where(line == 1, middle, jnp.where(line == 2, low, 0.0)))
    for turn, piece in enumerate(pieces):
        start = pl.multiple_of(((base[0] + turn) & 3) * quarter, quarter)
        piece[:electrons, :] = total[:, pl.ds(start, quarter)].astype(piece.dtype)
        if piece.dtype == jnp.float32:
            piece[electrons:, :] = energy[:8]
        else:
            piece[electrons:, :] = parts.astype(piece.dtype)


def close(base, zero, one, two, three, green):
    electrons, orbitals = zero.shape
    vmem = pl.BlockSpec(memory_space=pltpu.VMEM)
    return pl.pallas_call(
        close_kernel,
        out_shape=[
            jax.ShapeDtypeStruct((electrons + lines, orbitals // 4), kind)
            for lines, kind in zip(NOTE, KINDS)
        ],
        in_specs=[pl.BlockSpec(memory_space=pltpu.SMEM)] + [vmem] * 5,
        out_specs=[vmem] * 4,
        scratch_shapes=[pltpu.VMEM((electrons, orbitals), jnp.float32)],
        compiler_params=pltpu.CompilerParams(vmem_limit_bytes=8 << 20),
        name="close",
    )(base, zero, one, two, three, green)


def finish_kernel(root, factor, p0, p1, p2, p3, gradient, energy):
    electrons = gradient.shape[1]
    total, note = 0.0, 0.0
    for piece in (p0, p1, p2, p3):
        total = total + piece[:electrons, :].astype(jnp.float32)
        if piece.dtype == jnp.float32:
            note = note + piece[electrons : electrons + 1, :]
        else:
            note = note + jnp.sum(piece[electrons:, :].astype(jnp.float32), axis=0, keepdims=True)
    gradient[0] = total / root
    energy[0] = jnp.max(note) * factor


def finish(pieces, root, factor):
    electrons = pieces[0].shape[0] - NOTE[0]
    vmem = pl.BlockSpec(memory_space=pltpu.VMEM)
    return pl.pallas_call(
        functools.partial(finish_kernel, root, factor),
        out_shape=[
            jax.ShapeDtypeStruct((1, electrons, pieces[0].shape[1]), jnp.float32),
            jax.ShapeDtypeStruct((1,), jnp.float32),
        ],
        in_specs=[vmem] * 4,
        out_specs=[vmem, pl.BlockSpec(memory_space=pltpu.SMEM)],
        compiler_params=pltpu.CompilerParams(vmem_limit_bytes=8 << 20),
        name="finish",
    )(*pieces)


def shards(cholesky_factors, walker_green):
    f32, bf16 = jnp.float32, jnp.bfloat16
    blk_count = lax.axis_size("blk")
    vec_count = lax.axis_size("vec")
    vector_total = cholesky_factors.shape[0] * blk_count * vec_count
    electrons, _ = walker_green.shape[1:]
    vec = lax.axis_index("vec")
    core = vec % 2
    x_lo = lax.axis_index("blk") // 16
    x_hi = vec // 2

    partner = send(cholesky_factors, SWAP)
    across = send(walker_green, first(2, -1))
    ahead = send(walker_green, first(-1, -1))
    behind = send(walker_green, first(1, 1))
    green = send(walker_green, first(0, 1))
    row_a = pair(ahead, across)
    row_b = pair(behind, green)
    vectors = lax.optimization_barrier(joined(cholesky_factors, partner))
    ahead_a = send(row_a, along_s(-1))
    behind_b = send(row_b, along_s(1))
    own = intersect(vectors, joined(across, behind, ahead, green))
    far_a = send(ahead_a, along_s(-1))
    far_b = send(behind_b, along_s(1))
    y_terms = terms(vectors, intersect(vectors, joined(ahead_a, behind_b)), f32)
    ahead_b = send(row_b, along_s(-1))
    behind_a = send(row_a, along_s(1))
    far_terms = terms(vectors, intersect(vectors, joined(far_a, far_b)))
    via_a = send(far_terms[:2], along_s(1))
    via_b = send(far_terms[2:], along_s(-1))
    x_terms = terms(vectors, intersect(vectors, joined(ahead_b, behind_a)))
    y_ahead = (y_terms[:2] + via_a.astype(f32)).astype(bf16)
    y_behind = (y_terms[2:] + via_b.astype(f32)).astype(bf16)
    ahead_1 = send(jnp.stack([y_ahead[1], x_terms[0]]), along_s(1))
    behind_1 = send(jnp.stack([x_terms[3], y_behind[0]]), along_s(-1))
    ahead_2 = send(jnp.stack([y_ahead[0], x_terms[1]]), along_s(1))
    behind_2 = send(jnp.stack([x_terms[2], y_behind[1]]), along_s(-1))

    total = terms(vectors, own, f32)
    early = (total[:2] + ahead_1.astype(f32) + behind_1.astype(f32)).astype(bf16)
    total, _ = lax.optimization_barrier((total[2:], early))
    two = send(early[0], along_f(2))
    three = send(early[1], along_f(-1))
    total = total + ahead_2.astype(f32) + behind_2.astype(f32)
    one = send(total[0].astype(bf16), along_f(1))
    zero = total[1]
    base = (2 * x_hi + x_lo + 4 - (x_lo ^ core)) & 3
    pieces = close(base.reshape(1), zero, one, two, three, green[0])
    pieces = [send(pieces[turn], last(turn)) for turn in range(4)]
    gradient, energy = finish(pieces, math.sqrt(vector_total), -0.5 / (electrons * vector_total))
    return (gradient, energy)


def solution(mesh):
    return jax.shard_map(
        shards,
        mesh=mesh,
        in_specs=(P(("blk", "vec"), None, None), P("blk", None, None)),
        out_specs=(P("blk", None, "vec"), P("blk")),
        check_vma=False,
    )
```

```python
import functools
import math

import jax
import jax.numpy as jnp
from jax import lax
from jax.experimental import pallas as pl
from jax.experimental.pallas import tpu as pltpu
from jax.sharding import PartitionSpec as P


AXES = ("blk", "vec")
CHIPS = [(x, y, z, c) for x in range(4) for y in range(4) for z in range(4) for c in range(2)]


def place(x, y, z, c):
    x, y, z = x % 4, y % 4, z % 4
    return ((x % 2) * 16 + z * 4 + y) * 4 + (x // 2) * 2 + c


def route(target, chosen=lambda x, y, z, c: True):
    return [(place(*d), place(*target(*d))) for d in CHIPS if chosen(*d)]


def along_f(step):
    return route(lambda x, y, z, c: (x, y, z + step, c) if c else (x, y + step, z, c))


def along_s(step):
    return route(lambda x, y, z, c: (x, y + step, z, c) if c else (x, y, z + step, c))


SWAP = route(lambda x, y, z, c: (x, y, z, 1 - c))


def first(step, side):
    return route(lambda x, y, z, c: (x + side, y, z + step, c) if c else (x, y + step, z, c))


def goal(turn, x, c):
    return (x - (x + c) % 2 + turn) % 4


def last(turn):
    def target(x, y, z, c):
        half, core = goal(turn, x, c) // 2, goal(turn, x, c) % 2
        return 2 * half + (x + c) % 2, y, z, core

    return route(target)


def send(value, pairs):
    return lax.ppermute(value, AXES, pairs)


def joined(*parts):
    return jnp.concatenate(parts, axis=0)


def intersect(vectors, greens):
    part = jnp.einsum("gap,wbp->wgab", vectors, greens, preferred_element_type=jnp.float32)
    part = part.astype(jnp.bfloat16)
    return lax.optimization_barrier(part)


def terms(vectors, part, kind=jnp.bfloat16):
    total = jnp.einsum("wglr,grm->wlm", part, vectors, preferred_element_type=jnp.float32)
    total = total.astype(kind)
    return lax.optimization_barrier(total)


KINDS = (jnp.float32, jnp.float32, jnp.bfloat16, jnp.bfloat16)
NOTE = (8, 8, 16, 16)


def pair_kernel(first_ref, second_ref, out_ref):
    out_ref[:1] = first_ref[...]
    out_ref[1:] = second_ref[...]


def pair(one, two):
    vmem = pl.BlockSpec(memory_space=pltpu.VMEM)
    return pl.pallas_call(
        pair_kernel,
        out_shape=jax.ShapeDtypeStruct((2, *one.shape[1:]), one.dtype),
        in_specs=[vmem] * 2,
        out_specs=vmem,
        compiler_params=pltpu.CompilerParams(vmem_limit_bytes=8 << 20),
        name="pair",
    )(one, two)


def close_kernel(base, zero, one, two, three, green, *rest):
    pieces, total = rest[:4], rest[4]
    electrons, orbitals = zero.shape
    quarter = orbitals // 4
    products = jnp.zeros((electrons, quarter), jnp.float32)
    for column in range(4):
        block = slice(column * quarter, (column + 1) * quarter)
        value = zero[:, block] + one[:, block].astype(jnp.float32)
        value = value + two[:, block].astype(jnp.float32) + three[:, block].astype(jnp.float32)
        total[:, block] = value
        products = products + value * green[:, block].astype(jnp.float32)
    energy = jnp.full((16, quarter), jnp.sum(products), jnp.float32)
    high = energy.astype(jnp.bfloat16).astype(jnp.float32)
    middle = (energy - high).astype(jnp.bfloat16).astype(jnp.float32)
    low = energy - high - middle
    line = lax.broadcasted_iota(jnp.int32, energy.shape, 0)
    parts = jnp.where(line == 0, high, jnp.where(line == 1, middle, jnp.where(line == 2, low, 0.0)))
    for turn, piece in enumerate(pieces):
        start = pl.multiple_of(((base[0] + turn) & 3) * quarter, quarter)
        piece[:electrons, :] = total[:, pl.ds(start, quarter)].astype(piece.dtype)
        if piece.dtype == jnp.float32:
            piece[electrons:, :] = energy[:8]
        else:
            piece[electrons:, :] = parts.astype(piece.dtype)


def close(base, zero, one, two, three, green):
    electrons, orbitals = zero.shape
    vmem = pl.BlockSpec(memory_space=pltpu.VMEM)
    return pl.pallas_call(
        close_kernel,
        out_shape=[
            jax.ShapeDtypeStruct((electrons + lines, orbitals // 4), kind)
            for lines, kind in zip(NOTE, KINDS)
        ],
        in_specs=[pl.BlockSpec(memory_space=pltpu.SMEM)] + [vmem] * 5,
        out_specs=[vmem] * 4,
        scratch_shapes=[pltpu.VMEM((electrons, orbitals), jnp.float32)],
        compiler_params=pltpu.CompilerParams(vmem_limit_bytes=8 << 20),
        name="close",
    )(base, zero, one, two, three, green)


def finish_kernel(root, factor, p0, p1, p2, p3, gradient, energy):
    electrons = gradient.shape[1]
    total, note = 0.0, 0.0
    for piece in (p0, p1, p2, p3):
        total = total + piece[:electrons, :].astype(jnp.float32)
        if piece.dtype == jnp.float32:
            note = note + piece[electrons : electrons + 1, :]
        else:
            note = note + jnp.sum(piece[electrons:, :].astype(jnp.float32), axis=0, keepdims=True)
    gradient[0] = total / root
    energy[0] = jnp.max(note) * factor


def finish(pieces, root, factor):
    electrons = pieces[0].shape[0] - NOTE[0]
    vmem = pl.BlockSpec(memory_space=pltpu.VMEM)
    return pl.pallas_call(
        functools.partial(finish_kernel, root, factor),
        out_shape=[
            jax.ShapeDtypeStruct((1, electrons, pieces[0].shape[1]), jnp.float32),
            jax.ShapeDtypeStruct((1,), jnp.float32),
        ],
        in_specs=[vmem] * 4,
        out_specs=[vmem, pl.BlockSpec(memory_space=pltpu.SMEM)],
        compiler_params=pltpu.CompilerParams(vmem_limit_bytes=8 << 20),
        name="finish",
    )(*pieces)


def shards(cholesky_factors, walker_green):
    f32, bf16 = jnp.float32, jnp.bfloat16
    blk_count = lax.axis_size("blk")
    vec_count = lax.axis_size("vec")
    vector_total = cholesky_factors.shape[0] * blk_count * vec_count
    electrons, _ = walker_green.shape[1:]
    vec = lax.axis_index("vec")
    core = vec % 2
    x_lo = lax.axis_index("blk") // 16
    x_hi = vec // 2

    partner = send(cholesky_factors, SWAP)
    across = send(walker_green, first(2, -1))
    ahead = send(walker_green, first(-1, -1))
    behind = send(walker_green, first(1, 1))
    green = send(walker_green, first(0, 1))
    row_a = pair(ahead, across)
    row_b = pair(behind, green)
    vectors = lax.optimization_barrier(joined(cholesky_factors, partner))
    ahead_a = send(row_a, along_s(-1))
    behind_b = send(row_b, along_s(1))
    own = intersect(vectors, joined(across, behind, ahead, green))
    far_a = send(ahead_a, along_s(-1))
    far_b = send(behind_b, along_s(1))
    y_terms = terms(vectors, intersect(vectors, joined(ahead_a, behind_b)), f32)
    ahead_b = send(row_b, along_s(-1))
    behind_a = send(row_a, along_s(1))
    far_terms = terms(vectors, intersect(vectors, joined(far_a, far_b)))
    via_a = send(far_terms[:2], along_s(1))
    via_b = send(far_terms[2:], along_s(-1))
    x_terms = terms(vectors, intersect(vectors, joined(ahead_b, behind_a)))
    y_ahead = (y_terms[:2] + via_a.astype(f32)).astype(bf16)
    y_behind = (y_terms[2:] + via_b.astype(f32)).astype(bf16)
    ahead_1 = send(jnp.stack([y_ahead[1], x_terms[0], y_ahead[0]]), along_s(1))
    behind_1 = send(jnp.stack([x_terms[3], y_behind[0], x_terms[2]]), along_s(-1))
    ahead_2 = send(x_terms[1], along_s(1))
    behind_2 = send(y_behind[1], along_s(-1))

    total = terms(vectors, own, f32)
    early = (total[:3] + ahead_1.astype(f32) + behind_1.astype(f32)).astype(bf16)
    zero, _ = lax.optimization_barrier((total[3], early))
    two = send(early[0], along_f(2))
    three = send(early[1], along_f(-1))
    one = send(early[2], along_f(1))
    zero = zero + ahead_2.astype(f32) + behind_2.astype(f32)
    base = (2 * x_hi + x_lo + 4 - (x_lo ^ core)) & 3
    pieces = close(base.reshape(1), zero, one, two, three, green[0])
    pieces = [send(pieces[turn], last(turn)) for turn in range(4)]
    gradient, energy = finish(pieces, math.sqrt(vector_total), -0.5 / (electrons * vector_total))
    return (gradient, energy)


def solution(mesh):
    return jax.shard_map(
        shards,
        mesh=mesh,
        in_specs=(P(("blk", "vec"), None, None), P("blk", None, None)),
        out_specs=(P("blk", None, "vec"), P("blk")),
        check_vma=False,
    )
```
